32 devices in a mesh: rep: 2 (over y), seq: 4 (over x, core), head: 4 (over z).
Axes of the slice: x: 2, y: 2, z: 4, core: 2. Of those that a mesh axis runs over, the one named last changes fastest.
Arguments:
- query: bfloat16 [32768, 2048], P(('rep', 'seq', 'head')), parts along dimension 0, may hold values from -6 to 6
- key: bfloat16 [32768, 2048], P(('rep', 'seq', 'head')), parts along dimension 0, may hold values from -6 to 6
- value: bfloat16 [32768, 2048], P(('rep', 'seq', 'head')), parts along dimension 0, may hold values from -6 to 6
- grad_out: bfloat16 [32768, 2048], P(('rep', 'seq', 'head')), parts along dimension 0, may hold values from -6 to 6
- level_weights: bfloat16 [32768, 128], P(('rep', 'seq', 'head')), parts along dimension 0, may hold values from 0.25 to 4
Outputs:
- attended: bfloat16 [32768, 2048], P(('rep', 'seq', 'head')), parts along dimension 0
- grad_query: bfloat16 [32768, 2048], P(('rep', 'seq', 'head')), parts along dimension 0
- grad_key: bfloat16 [32768, 2048], P(('rep', 'seq', 'head')), parts along dimension 0
- grad_value: bfloat16 [32768, 2048], P(('rep', 'seq', 'head')), parts along dimension 0
- grad_weights: bfloat16 [32768, 128], P(('rep', 'seq', 'head')), parts along dimension 0
The draws below stay inside these ranges and needn't reach their ends.
There are 2 independent parts, one for each index of `rep`. The reference program is written for one: setup_inputs(seed, part) draws one part's arguments, and reference() takes and returns one part's arrays. A program takes and returns all parts, laid end to end along the dimension named above; each array names one. Nothing has to cross between parts.
All inputs are finite; a program needn't handle non-finite values.
Results may differ from the reference program's by a relative error of at most 0.0056.
Values may be sent and summed in bfloat16 or wider, within the bound.
A program may use at most 384 MiB of HBM per device.

```python
import math
import jax
import jax.numpy as jnp
from jax import lax

H = 16
DH = 128
C = 128
LEVELS = 8
WIDTH = 2048
NC = 128
TOKENS = 16384


def steps_of(own_key, shape, pieces, low, top_value):
    loudness, own = 1.0, jax.random.fold_in(own_key, 6)
    for dim, shards_of in pieces:
        heights = jnp.exp(jax.random.uniform(jax.random.fold_in(own, dim), (shards_of,), jnp.float32, low / len(pieces), top_value / len(pieces)))
        loudness = loudness * jnp.repeat(heights, shape[dim] // shards_of).reshape([-1 if axis == dim else 1 for axis in range(len(shape))])
    return loudness


def scatter_about(own_key, extent, spread, limit, split=(), kind=jnp.bfloat16):
    loudness = steps_of(own_key, extent, split, -0.22, 0.18) if split else 1.0
    entries = jax.random.normal(own_key, extent, jnp.float32) * spread * loudness
    return jnp.minimum(jnp.maximum(entries, -limit), limit).astype(kind)


def setup_inputs(seed: int = 0, part: int = 0) -> dict:
    key_list = jax.random.split(jax.random.key(seed), 6)
    own_keys = jax.random.split(jax.random.fold_in(key_list[5], part), 6)
    return {
        "query": scatter_about(own_keys[0], (TOKENS, WIDTH), 1.0, 6.0, ((0, 16),)),
        "key": scatter_about(own_keys[1], (TOKENS, WIDTH), 1.0, 6.0, ((0, 16),)),
        "value": scatter_about(own_keys[2], (TOKENS, WIDTH), 1.0, 6.0, ((0, 16),)),
        "grad_out": scatter_about(own_keys[3], (TOKENS, WIDTH), 1.0, 6.0, ((0, 16),)),
        "level_weights": jnp.clip(jnp.exp(math.log(4.0) - 2.7725887 * jax.random.uniform(own_keys[4], (TOKENS, H * LEVELS), jnp.float32) ** steps_of(own_keys[4], (TOKENS, H * LEVELS), ((0, 16),), -0.2, 0.2)), 0.25, 4.0).astype(jnp.bfloat16),
    }


def level_scale(level):
    if level == 0:
        return 1.0 / math.sqrt(DH * C)
    return 1.0 / math.sqrt(DH * C * 2 ** (level - 1))

def bucket_matrix(count, level_bit):
    rows = jnp.arange(count, dtype=jnp.int32)[:, None]
    columns = jnp.arange(count, dtype=jnp.int32)[None, :]
    stride = 2 ** level_bit
    reading = rows // stride % 2 == 1
    inside = columns // stride == rows // (2 * stride) * 2
    return jnp.where(reading & inside, 1.0, 0.0).astype(jnp.float32)

def rounded(values):
    return lax.optimization_barrier(values.astype(jnp.bfloat16)).astype(jnp.float32)

def one_head(inputs):
    query, key, value, grad_out, weights = inputs
    query_full = query.astype(jnp.float32)
    key_full = key.astype(jnp.float32)
    value_full = value.astype(jnp.float32)
    grad_full = grad_out.astype(jnp.float32)
    mask = jnp.tril(jnp.ones((C, C), jnp.float32))
    scores = jnp.einsum('ntd,nsd->nts', query_full, key_full) * level_scale(0) * mask
    first = weights[:, :, 0:1]
    probs = rounded(first * scores)
    attended = jnp.einsum('nts,nsd->ntd', probs, value_full)
    grad_probs = jnp.einsum('nte,nse->nts', grad_full, value_full)
    grad_levels = [lax.optimization_barrier(jnp.sum(scores * grad_probs, axis=-1))]
    grad_scores = rounded(first * grad_probs * level_scale(0) * mask)
    grad_query = jnp.einsum('nts,nsd->ntd', grad_scores, key_full)
    grad_key = jnp.einsum('nts,ntd->nsd', grad_scores, query_full)
    grad_value = jnp.einsum('nts,nte->nse', probs, grad_full)
    states = jnp.einsum('nsd,nse->nde', key_full, value_full)
    adjoint = jnp.zeros((NC, DH, DH), jnp.float32)
    for level in range(1, LEVELS):
        mapping = bucket_matrix(NC, level - 1)
        summed = jnp.einsum('cj,jde->cde', mapping, states, precision=lax.Precision.HIGHEST)
        read_state = rounded(level_scale(level) * summed)
        reads = jnp.einsum('ntd,nde->nte', query_full, read_state)
        weight = weights[:, :, level:level + 1]
        attended = attended + weight * reads
        grad_levels.append(lax.optimization_barrier(jnp.sum(grad_full * reads, axis=-1)))
        grad_query = grad_query + weight * jnp.einsum('nte,nde->ntd', grad_full, read_state)
        weighted = rounded(weight * query_full)
        products = jnp.einsum('ntd,nte->nde', weighted, grad_full)
        adjoint = adjoint + level_scale(level) * jnp.einsum('cj,cde->jde', mapping, products, precision=lax.Precision.HIGHEST)
    adjoint_low = rounded(adjoint)
    grad_key = grad_key + jnp.einsum('nse,nde->nsd', value_full, adjoint_low)
    grad_value = grad_value + jnp.einsum('nsd,nde->nse', key_full, adjoint_low)
    return (attended.astype(jnp.bfloat16), grad_query.astype(jnp.bfloat16), grad_key.astype(jnp.bfloat16), grad_value.astype(jnp.bfloat16), jnp.stack(grad_levels, axis=-1).astype(jnp.bfloat16))

def split_heads(array, width):
    return array.reshape(NC, C, H, width).transpose(2, 0, 1, 3)

def join_heads(array):
    return array.transpose(1, 2, 0, 3).reshape(NC * C, array.shape[0] * array.shape[3])

def reference(query, key, value, grad_out, level_weights):
    inputs = (split_heads(query, DH), split_heads(key, DH), split_heads(value, DH), split_heads(grad_out, DH), split_heads(level_weights, LEVELS).astype(jnp.float32))
    results = lax.map(one_head, inputs)
    return (join_heads(results[0]), join_heads(results[1]), join_heads(results[2]), join_heads(results[3]), join_heads(results[4]))
```

```python
import functools
import math

import jax
import jax.numpy as jnp
from jax import lax
from jax.experimental import pallas as pl
from jax.experimental.pallas import tpu as pltpu
from jax.sharding import PartitionSpec as P

DH = 128
C = 128
LEVELS = 8
AXES = ("seq", "head")
VMEM_LIMIT = 50 * 2**20
BF = jnp.bfloat16
F32 = jnp.float32


def level_scale(level):
    if level == 0:
        return 1.0 / math.sqrt(DH * C)
    return 1.0 / math.sqrt(DH * C * 2 ** (level - 1))


def nn(a, b):
    return lax.dot_general(a, b, (((1,), (0,)), ((), ())), preferred_element_type=F32)


def nt(a, b):
    return lax.dot_general(a, b, (((1,), (1,)), ((), ())), preferred_element_type=F32)


def tn(a, b):
    return lax.dot_general(a, b, (((0,), (0,)), ((), ())), preferred_element_type=F32)


def cat(parts, axis):
    return parts[0] if len(parts) == 1 else jnp.concatenate(parts, axis=axis)


def head_weights(w_ref, head):
    width = w_ref.shape[1]
    return pltpu.roll(w_ref[...].astype(F32), lax.rem(width - head * LEVELS, width), 1)


def pick(rows, head, level, width):
    lane = lax.broadcasted_iota(jnp.int32, (rows, width), 1)
    return jnp.where(lane == head * LEVELS + level, 1.0, 0.0).astype(BF)


def sums_kernel(local_bits, q_ref, k_ref, v_ref, g_ref, w_ref, t_ref, *rest):
    p_refs, wr = rest[:-1], rest[-1]
    head = pl.program_id(0)
    wr[...] = head_weights(w_ref, head)
    t_ref[0] = tn(k_ref[...], v_ref[...]).astype(BF)
    q = q_ref[...].astype(F32)
    weighted = [
        (wr[:, local_bits + 1 + j : local_bits + 2 + j] * q).astype(BF) for j in range(len(p_refs))
    ]
    out = tn(g_ref[...], cat(weighted, 1))
    for j, p_ref in enumerate(p_refs):
        p_ref[0] = out[:, j * DH : (j + 1) * DH].astype(BF)


def sums_call(query, key, value, grad_out, weights, heads, local_bits, cross_bits):
    tokens = query.shape[0]
    column = pl.BlockSpec((tokens, DH), lambda h: (0, h))
    square = pl.BlockSpec((1, DH, DH), lambda h: (h, 0, 0))
    outs = [jax.ShapeDtypeStruct((heads, DH, DH), BF)] * (1 + cross_bits)
    return pl.pallas_call(
        functools.partial(sums_kernel, local_bits),
        grid=(heads,),
        in_specs=[column] * 4 + [pl.BlockSpec(weights.shape, lambda h: (0, 0))],
        out_specs=[square] * (1 + cross_bits),
        out_shape=outs,
        scratch_shapes=[pltpu.VMEM(weights.shape, F32)],
        compiler_params=pltpu.CompilerParams(vmem_limit_bytes=VMEM_LIMIT),
        name="sums",
    )(query, key, value, grad_out, weights)


def local_kernel(first_head, stretches, aliased, *refs):
    q_ref, k_ref, v_ref, g_ref, w_ref = refs[:5]
    att_ref, dq_ref, dk_ref, dv_ref, gw_ref, wr = refs[5 + aliased :]
    step = pl.program_id(0)
    head = first_head + step
    local_bits = stretches.bit_length() - 1
    width = w_ref.shape[1]

    @pl.when(step == 0)
    def _():
        gw_ref[...] = jnp.zeros_like(gw_ref)

    wr[...] = head_weights(w_ref, head)

    def rows(ref, n, count=1):
        return ref[n * C : (n + count) * C, :]

    def weighted(n, level):
        return (wr[n * C : (n + 1) * C, level : level + 1] * rows(q_ref, n).astype(F32)).astype(BF)

    sums = {}
    for n in range(stretches - 1):
        sums[0, n] = tn(rows(k_ref, n), rows(v_ref, n))
    for b in range(1, local_bits):
        for m in range(stretches >> b):
            if (b - 1, 2 * m + 1) in sums:
                sums[b, m] = sums[b - 1, 2 * m] + sums[b - 1, 2 * m + 1]
    states, adjoints, wq = {}, {}, {}
    for b in range(local_bits):
        for group in range(stretches >> (b + 1)):
            states[b, group] = (level_scale(b + 1) * sums[b, 2 * group]).astype(BF)
            first = (2 * group + 1) << b
            for n in range(first, first + (1 << b)):
                wq[b, n] = weighted(n, b + 1)
            up = cat([wq[b, n] for n in range(first, first + (1 << b))], 0)
            adjoints[b, group] = level_scale(b + 1) * tn(rows(g_ref, first, 1 << b), up)

    row = lax.broadcasted_iota(jnp.int32, (C, C), 0)
    col = lax.broadcasted_iota(jnp.int32, (C, C), 1)
    mask = jnp.where(col <= row, level_scale(0), 0.0).astype(F32)
    for n in range(stretches):
        q, k, v, g = (rows(ref, n) for ref in (q_ref, k_ref, v_ref, g_ref))
        here = slice(n * C, (n + 1) * C)
        bits = [b for b in range(local_bits) if n >> b & 1]
        read = [states[b, n >> (b + 1)] for b in bits]
        scores = nt(q, k) * mask
        grads = nt(g, v)
        w0 = wr[here, 0:1]
        probs = (w0 * scores).astype(BF)
        gscores = (w0 * (grads * mask)).astype(BF)
        att = nn(cat([probs] + [wq[b, n] for b in bits], 1), cat([v] + read, 0))
        dq = nn(gscores, k)
        marks = [(scores * grads).astype(BF)]
        q32 = q.astype(F32)
        for b, state in zip(bits, read):
            back = nt(g, state)
            dq = dq + wr[here, b + 1 : b + 2] * back
            marks.append((q32 * back).astype(BF))
        picks = [pick(C, head, level, width) for level in [0] + [b + 1 for b in bits]]
        gw_ref[here, :] += nn(cat(marks, 1), cat(picks, 0))
        dk = tn(gscores, q)
        dv = tn(probs, g)
        adjoint = None
        for b in range(local_bits):
            if not n >> b & 1:
                term = adjoints[b, n >> (b + 1)]
                adjoint = term if adjoint is None else adjoint + term
        if adjoint is not None:
            adjoint = adjoint.astype(BF)
            dk = dk + nn(v, adjoint)
            dv = dv + nt(k, adjoint)
        att_ref[here, :] = att.astype(BF)
        dq_ref[here, :] = dq.astype(BF)
        dk_ref[here, :] = dk.astype(BF)
        dv_ref[here, :] = dv.astype(BF)


def local_call(query, key, value, grad_out, weights, partial, first_head, count):
    tokens = query.shape[0]
    stretches = tokens // C
    column = pl.BlockSpec((tokens, DH), lambda h: (0, first_head + h))
    whole = pl.BlockSpec(weights.shape, lambda h: (0, 0))
    shape = jax.ShapeDtypeStruct(query.shape, BF)
    flops = 2 * count * stretches * 18 * C * C * C
    return pl.pallas_call(
        functools.partial(local_kernel, first_head, stretches, len(partial)),
        grid=(count,),
        in_specs=[column] * 4 + [whole] + [pl.BlockSpec(memory_space=pl.ANY)] * len(partial),
        out_specs=[column] * 4 + [whole],
        out_shape=[shape] * 4 + [jax.ShapeDtypeStruct(weights.shape, F32)],
        scratch_shapes=[pltpu.VMEM(weights.shape, F32)],
        input_output_aliases={5 + i: i for i in range(len(partial))},
        compiler_params=pltpu.CompilerParams(vmem_limit_bytes=VMEM_LIMIT),
        cost_estimate=pl.CostEstimate(
            flops=flops * 8, bytes_accessed=count * tokens * DH * 16, transcendentals=0
        ),
        name="local",
    )(query, key, value, grad_out, weights, *partial)


def cross_kernel(local_bits, cross_bits, chunks, *refs):
    q_ref, k_ref, v_ref, g_ref, w_ref = refs[:5]
    att_in, dq_in, dk_in, dv_in = refs[5:9]
    gw_in = refs[9 : 9 + chunks]
    states = refs[9 + chunks : 9 + chunks + cross_bits]
    adjoint = refs[9 + chunks + cross_bits]
    att_ref, dq_ref, dk_ref, dv_ref, gw_ref, acc, wr = refs[10 + chunks + cross_bits :]
    head = pl.program_id(0)
    width = w_ref.shape[1]

    @pl.when(head == 0)
    def _():
        total = gw_in[0][...]
        for other in gw_in[1:]:
            total = total + other[...]
        acc[...] = total

    wr[...] = head_weights(w_ref, head)
    read = cat([state[0] for state in states], 0)
    adj = adjoint[0]
    picks = cat([pick(DH, head, local_bits + 1 + j, width) for j in range(cross_bits)], 0)
    tokens = q_ref.shape[0]
    step = min(2 * C, tokens)
    for start in range(0, tokens, step):
        here = slice(start, start + step)
        q32 = q_ref[here, :].astype(F32)
        columns = [
            wr[here, local_bits + 1 + j : local_bits + 2 + j] for j in range(cross_bits)
        ]
        att = att_in[here, :].astype(F32) + nn(cat([(w * q32).astype(BF) for w in columns], 1), read)
        back = nt(g_ref[here, :], read)
        dq = dq_in[here, :].astype(F32)
        marks = []
        for j, w in enumerate(columns):
            part = back[:, j * DH : (j + 1) * DH]
            dq = dq + w * part
            marks.append((q32 * part).astype(BF))
        acc[here, :] += nn(cat(marks, 1), picks)
        att_ref[here, :] = att.astype(BF)
        dq_ref[here, :] = dq.astype(BF)
        dk_ref[here, :] = (dk_in[here, :].astype(F32) + nn(v_ref[here, :], adj)).astype(BF)
        dv_ref[here, :] = (dv_in[here, :].astype(F32) + nt(k_ref[here, :], adj)).astype(BF)

    @pl.when(head == pl.num_programs(0) - 1)
    def _():
        gw_ref[...] = acc[...].astype(BF)


def cross_call(query, key, value, grad_out, weights, partial, gws, states, adjoint, local_bits):
    tokens = query.shape[0]
    heads = query.shape[1] // DH
    cross_bits = len(states)
    column = pl.BlockSpec((tokens, DH), lambda h: (0, h))
    whole = pl.BlockSpec(weights.shape, lambda h: (0, 0))
    square = pl.BlockSpec((1, DH, DH), lambda h: (h, 0, 0))
    return pl.pallas_call(
        functools.partial(cross_kernel, local_bits, cross_bits, len(gws)),
        grid=(heads,),
        in_specs=[column] * 4
        + [whole]
        + [column] * 4
        + [whole] * len(gws)
        + [square] * (cross_bits + 1),
        out_specs=[column] * 4 + [whole],
        out_shape=[jax.ShapeDtypeStruct(query.shape, BF)] * 4
        + [jax.ShapeDtypeStruct(weights.shape, BF)],
        scratch_shapes=[pltpu.VMEM(weights.shape, F32), pltpu.VMEM(weights.shape, F32)],
        input_output_aliases={5 + i: i for i in range(4)},
        compiler_params=pltpu.CompilerParams(vmem_limit_bytes=VMEM_LIMIT),
        name="cross",
    )(query, key, value, grad_out, weights, *partial, *gws, *states, adjoint)


def exchange(total, products, local_bits):
    devices = lax.axis_size(AXES)
    me = lax.axis_index(AXES)
    cross_bits = devices.bit_length() - 1
    products = [product for product in products]
    states = []
    adjoint = None
    for i in range(cross_bits):
        stride = 1 << i
        pairs = [(p, p ^ stride) for p in range(devices)]
        if i == cross_bits - 1:
            pairs = [(p, r) for p, r in pairs if p < r]
        other = lax.ppermute(total.astype(BF), AXES, pairs).astype(F32)
        down = [(p, p ^ stride) for p in range(devices) if p & stride]
        term = level_scale(local_bits + i + 1) * lax.ppermute(
            products[i].astype(BF), AXES, down
        ).astype(F32)
        adjoint = term if adjoint is None else adjoint + term
        for j in range(i + 1, cross_bits):
            upper = [(p, p ^ stride) for p in range(devices) if p >> j & 1]
            products[j] = products[j].astype(F32) + lax.ppermute(
                products[j].astype(BF), AXES, upper
            ).astype(F32)
        reads = me // stride % 2 == 1
        states.append(
            jnp.where(reads, level_scale(local_bits + i + 1) * other, 0.0).astype(BF)
        )
        total = total.astype(F32) + other
    return states, adjoint.astype(BF)


def shards(query, key, value, grad_out, weights):
    tokens = query.shape[0]
    heads = query.shape[1] // DH
    stretches = tokens // C
    local_bits = stretches.bit_length() - 1
    cross_bits = LEVELS - 1 - local_bits
    total, *products = sums_call(
        query, key, value, grad_out, weights, heads, local_bits, cross_bits
    )
    chunks = min(4, heads)
    count = heads // chunks
    partial, gws = [], []
    for c in range(chunks):
        *partial, gw = local_call(
            query, key, value, grad_out, weights, partial, c * count, count
        )
        gws.append(gw)
    states, adjoint = exchange(total, products, local_bits)
    return tuple(
        cross_call(
            query, key, value, grad_out, weights, partial, gws, states, adjoint, local_bits
        )
    )


def solution(mesh):
    spec = P(("rep", "seq", "head"), None)
    return jax.shard_map(
        shards, mesh=mesh, in_specs=(spec,) * 5, out_specs=(spec,) * 5, check_vma=False
    )
```

```python
import functools
import math

import jax
import jax.numpy as jnp
from jax import lax
from jax.experimental import pallas as pl
from jax.experimental.pallas import tpu as pltpu
from jax.sharding import PartitionSpec as P

DH = 128
C = 128
LEVELS = 8
VMEM_LIMIT = 60 * 2**20
BF = jnp.bfloat16
F32 = jnp.float32


def level_scale(level):
    if level == 0:
        return 1.0 / math.sqrt(DH * C)
    return 1.0 / math.sqrt(DH * C * 2 ** (level - 1))


def nn(a, b):
    return lax.dot_general(a, b, (((1,), (0,)), ((), ())), preferred_element_type=F32)


def nt(a, b):
    return lax.dot_general(a, b, (((1,), (1,)), ((), ())), preferred_element_type=F32)


def tn(a, b):
    return lax.dot_general(a, b, (((0,), (0,)), ((), ())), preferred_element_type=F32)


def cat(parts, axis):
    return parts[0] if len(parts) == 1 else jnp.concatenate(parts, axis=axis)


def head_weights(w_ref, head):
    width = w_ref.shape[1]
    return pltpu.roll(w_ref[...].astype(F32), lax.rem(width - head * LEVELS, width), 1)


def pick(rows, head, level, width):
    lane = lax.broadcasted_iota(jnp.int32, (rows, width), 1)
    return jnp.where(lane == head * LEVELS + level, 1.0, 0.0).astype(BF)


def sums_kernel(local_bits, q_ref, k_ref, v_ref, g_ref, w_ref, t_ref, *rest):
    p_refs, wr = rest[:-1], rest[-1]
    head = pl.program_id(0)
    wr[...] = head_weights(w_ref, head)
    t_ref[0] = tn(k_ref[...], v_ref[...]).astype(BF)
    q = q_ref[...].astype(F32)
    weighted = [
        (wr[:, local_bits + 1 + j : local_bits + 2 + j] * q).astype(BF) for j in range(len(p_refs))
    ]
    out = tn(g_ref[...], cat(weighted, 1))
    for j, p_ref in enumerate(p_refs):
        p_ref[0] = out[:, j * DH : (j + 1) * DH].astype(BF)


def sums_call(query, key, value, grad_out, weights, heads, local_bits, cross_bits):
    tokens = query.shape[0]
    column = pl.BlockSpec((tokens, DH), lambda h: (0, h))
    square = pl.BlockSpec((1, DH, DH), lambda h: (h, 0, 0))
    outs = [jax.ShapeDtypeStruct((heads, DH, DH), BF)] * (1 + cross_bits)
    return pl.pallas_call(
        functools.partial(sums_kernel, local_bits),
        grid=(heads,),
        in_specs=[column] * 4 + [pl.BlockSpec(weights.shape, lambda h: (0, 0))],
        out_specs=[square] * (1 + cross_bits),
        out_shape=outs,
        scratch_shapes=[pltpu.VMEM(weights.shape, F32)],
        compiler_params=pltpu.CompilerParams(vmem_limit_bytes=VMEM_LIMIT),
        name="sums",
    )(query, key, value, grad_out, weights)


class Exchange:
    def __init__(self, local_bits, cross_bits, head_bits, heads, chunks):
        self.local_bits, self.cross_bits, self.head_bits = local_bits, cross_bits, head_bits
        self.chunks, self.count = chunks, heads // chunks
        self.heads = heads
        self.received = cross_bits + cross_bits * (cross_bits + 1) // 2
        self.sent = cross_bits - 1 + cross_bits * (cross_bits - 1) // 2
        span = heads - chunks - 3
        last = max(cross_bits - 1, 1)
        self.offsets = [heads - chunks - (cross_bits - 1 - i) * span // last for i in range(cross_bits)]

    def scratch(self):
        sems = pltpu.SemaphoreType.DMA((self.received, self.chunks))
        return [
            pltpu.VMEM((self.received, self.heads, DH, DH), BF),
            pltpu.VMEM((max(self.sent, 1), self.heads, DH, DH), BF),
            pltpu.VMEM((self.heads, DH, DH), F32),
            sems,
            sems,
        ]

    def bind(self, sources, states, adjoint, scratch):
        self.sources, self.states, self.adjoint = sources, states, adjoint
        self.landing, self.sending, self.total, self.send_sem, self.recv_sem = scratch
        head, seq = lax.axis_index("head"), lax.axis_index("seq")
        self.bits, self.partners = [], []
        for i in range(self.cross_bits):
            name, position, stride = "head", head, 1 << i
            if i >= self.head_bits:
                name, position, stride = "seq", seq, 1 << (i - self.head_bits)
            bit = (position // stride) % 2
            self.bits.append(bit)
            self.partners.append({name: position + (1 - 2 * bit) * stride})

    def slot(self, item, i):
        return i if item == 0 else self.cross_bits + (item - 1) * item // 2 + i

    def source(self, item, i):
        if i == 0:
            return self.sources[item]
        j = item - 1
        return self.sending.at[i - 1 if item == 0 else self.cross_bits - 1 + j * (j - 1) // 2 + i - 1]

    def items(self, i):
        last = i == self.cross_bits - 1
        set_here, clear_here = self.bits[i] == 1, self.bits[i] == 0
        yield (0, clear_here, set_here) if last else (0, None, None)
        yield i + 1, set_here, clear_here
        for j in range(i + 1, self.cross_bits):
            yield j + 1, self.bits[j] == 1, self.bits[j] == 1

    def copy(self, item, i, chunk):
        part = pl.ds(chunk * self.count, self.count)
        slot = self.slot(item, i)
        return pltpu.make_async_remote_copy(
            src_ref=self.source(item, i).at[part],
            dst_ref=self.landing.at[slot, part],
            send_sem=self.send_sem.at[slot, chunk],
            recv_sem=self.recv_sem.at[slot, chunk],
            device_id=self.partners[i],
            device_id_type=pl.DeviceIdType.MESH,
        )

    def when(self, condition, body):
        if condition is None:
            body()
        else:
            pl.when(condition)(body)

    def start(self, i, chunk):
        for item, sends, _ in self.items(i):
            self.when(sends, lambda item=item: self.copy(item, i, chunk).start())

    def greet(self):
        barrier = pltpu.get_barrier_semaphore()
        for partner in self.partners:
            pl.semaphore_signal(
                barrier, inc=1, device_id=partner, device_id_type=pl.DeviceIdType.MESH
            )
        pl.semaphore_wait(barrier, self.cross_bits)

        def body(chunk, carry):
            self.start(0, chunk)
            return carry

        lax.fori_loop(0, self.chunks, body, 0)

    def arrive(self, i, chunk):
        part = pl.ds(chunk * self.count, self.count)
        shape = (self.count, DH, DH)
        factor = level_scale(self.local_bits + i + 1)
        last = i == self.cross_bits - 1

        def landed(item):
            return self.landing[self.slot(item, i), part].astype(F32)

        def add(item):
            self.source(item, i + 1)[part] = (
                self.source(item, i)[part].astype(F32) + landed(item)
            ).astype(BF)

        for item, _, receives in self.items(i):
            self.when(receives, lambda item=item: self.copy(item, i, chunk).wait_recv())
            if item == 0:
                if not last:
                    add(0)
            elif item == i + 1:
                continue
            else:
                self.when(receives, lambda item=item: add(item))
        if not last:
            self.start(i + 1, chunk)

        @pl.when(self.bits[i] == 1)
        def _():
            self.states[i][part] = (factor * landed(0)).astype(BF)
            if i == 0:
                self.total[part] = jnp.zeros(shape, F32)

        @pl.when(self.bits[i] == 0)
        def _():
            self.states[i][part] = jnp.zeros(shape, BF)
            if i == 0:
                self.total[part] = factor * landed(i + 1)
            else:
                self.total[part] += factor * landed(i + 1)

        if last:
            self.adjoint[part] = self.total[part].astype(BF)

    def advance(self, step):
        pl.when(step == 0)(self.greet)
        for i in reversed(range(self.cross_bits)):
            chunk = step - self.offsets[i]

            @pl.when((chunk >= 0) & (chunk < self.chunks))
            def _(i=i, chunk=chunk):
                self.arrive(i, chunk)

    def finish(self):
        def body(chunk, carry):
            for i in range(self.cross_bits):
                for item, sends, _ in self.items(i):
                    self.when(
                        sends, lambda item=item, i=i: self.copy(item, i, chunk).wait_send()
                    )
            return carry

        lax.fori_loop(0, self.chunks, body, 0)


def local_kernel(stretches, exchange, *refs):
    cross_bits = exchange.cross_bits
    q_ref, k_ref, v_ref, g_ref, w_ref = refs[:5]
    sources = refs[5 : 6 + cross_bits]
    outs = refs[6 + cross_bits :]
    att_ref, dq_ref, dk_ref, dv_ref, gw_ref = outs[:5]
    states_out = outs[5 : 5 + cross_bits]
    adjoint_out, wr = outs[5 + cross_bits : 7 + cross_bits]
    exchange.bind(sources, states_out, adjoint_out, outs[7 + cross_bits :])
    step = pl.program_id(0)
    head = step
    local_bits = stretches.bit_length() - 1
    width = w_ref.shape[1]

    @pl.when(step == 0)
    def _():
        gw_ref[...] = jnp.zeros_like(gw_ref)

    exchange.advance(step)
    wr[...] = head_weights(w_ref, head)

    def rows(ref, n, count=1):
        return ref[n * C : (n + count) * C, :]

    def weighted(n, level):
        return (wr[n * C : (n + 1) * C, level : level + 1] * rows(q_ref, n).astype(F32)).astype(BF)

    sums = {}
    for n in range(stretches - 1):
        sums[0, n] = tn(rows(k_ref, n), rows(v_ref, n))
    for b in range(1, local_bits):
        for m in range(stretches >> b):
            if (b - 1, 2 * m + 1) in sums:
                sums[b, m] = sums[b - 1, 2 * m] + sums[b - 1, 2 * m + 1]
    states, adjoints, wq = {}, {}, {}
    for b in range(local_bits):
        for group in range(stretches >> (b + 1)):
            states[b, group] = (level_scale(b + 1) * sums[b, 2 * group]).astype(BF)
            first = (2 * group + 1) << b
            for n in range(first, first + (1 << b)):
                wq[b, n] = weighted(n, b + 1)
            up = cat([wq[b, n] for n in range(first, first + (1 << b))], 0)
            adjoints[b, group] = level_scale(b + 1) * tn(rows(g_ref, first, 1 << b), up)

    row = lax.broadcasted_iota(jnp.int32, (C, C), 0)
    col = lax.broadcasted_iota(jnp.int32, (C, C), 1)
    mask = jnp.where(col <= row, level_scale(0), 0.0).astype(F32)
    for n in range(stretches):
        q, k, v, g = (rows(ref, n) for ref in (q_ref, k_ref, v_ref, g_ref))
        here = slice(n * C, (n + 1) * C)
        bits = [b for b in range(local_bits) if n >> b & 1]
        read = [states[b, n >> (b + 1)] for b in bits]
        scores = nt(q, k) * mask
        grads = nt(g, v)
        w0 = wr[here, 0:1]
        probs = (w0 * scores).astype(BF)
        gscores = (w0 * (grads * mask)).astype(BF)
        att = nn(cat([probs] + [wq[b, n] for b in bits], 1), cat([v] + read, 0))
        dq = nn(gscores, k)
        marks = [(scores * grads).astype(BF)]
        q32 = q.astype(F32)
        for b, state in zip(bits, read):
            back = nt(g, state)
            dq = dq + wr[here, b + 1 : b + 2] * back
            marks.append((q32 * back).astype(BF))
        picks = [pick(C, head, level, width) for level in [0] + [b + 1 for b in bits]]
        gw_ref[here, :] += nn(cat(marks, 1), cat(picks, 0))
        dk = tn(gscores, q)
        dv = tn(probs, g)
        adjoint = None
        for b in range(local_bits):
            if not n >> b & 1:
                term = adjoints[b, n >> (b + 1)]
                adjoint = term if adjoint is None else adjoint + term
        if adjoint is not None:
            adjoint = adjoint.astype(BF)
            dk = dk + nn(v, adjoint)
            dv = dv + nt(k, adjoint)
        att_ref[here, :] = att.astype(BF)
        dq_ref[here, :] = dq.astype(BF)
        dk_ref[here, :] = dk.astype(BF)
        dv_ref[here, :] = dv.astype(BF)

    @pl.when(step == pl.num_programs(0) - 1)
    def _():
        exchange.finish()


def local_call(query, key, value, grad_out, weights, sums, head_bits):
    tokens = query.shape[0]
    stretches = tokens // C
    heads = query.shape[1] // DH
    cross_bits = len(sums) - 1
    exchange = Exchange(stretches.bit_length() - 1, cross_bits, head_bits, heads, 4)
    column = pl.BlockSpec((tokens, DH), lambda h: (0, h))
    whole = pl.BlockSpec(weights.shape, lambda h: (0, 0))
    squares = pl.BlockSpec((heads, DH, DH), lambda h: (0, 0, 0))
    shape = jax.ShapeDtypeStruct(query.shape, BF)
    square = jax.ShapeDtypeStruct((heads, DH, DH), BF)
    return pl.pallas_call(
        functools.partial(local_kernel, stretches, exchange),
        grid=(heads,),
        in_specs=[column] * 4 + [whole] + [squares] * (cross_bits + 1),
        out_specs=[column] * 4 + [whole] + [squares] * (cross_bits + 1),
        out_shape=[shape] * 4
        + [jax.ShapeDtypeStruct(weights.shape, F32)]
        + [square] * (cross_bits + 1),
        scratch_shapes=[pltpu.VMEM(weights.shape, F32)] + exchange.scratch(),
        compiler_params=pltpu.CompilerParams(
            vmem_limit_bytes=VMEM_LIMIT, collective_id=0, has_side_effects=True
        ),
        name="local",
    )(query, key, value, grad_out, weights, *sums)


def cross_kernel(local_bits, cross_bits, chunks, *refs):
    q_ref, k_ref, v_ref, g_ref, w_ref = refs[:5]
    att_in, dq_in, dk_in, dv_in = refs[5:9]
    gw_in = refs[9 : 9 + chunks]
    states = refs[9 + chunks : 9 + chunks + cross_bits]
    adjoint = refs[9 + chunks + cross_bits]
    att_ref, dq_ref, dk_ref, dv_ref, gw_ref, acc, wr = refs[10 + chunks + cross_bits :]
    head = pl.program_id(0)
    width = w_ref.shape[1]

    @pl.when(head == 0)
    def _():
        total = gw_in[0][...]
        for other in gw_in[1:]:
            total = total + other[...]
        acc[...] = total

    wr[...] = head_weights(w_ref, head)
    read = cat([state[0] for state in states], 0)
    adj = adjoint[0]
    picks = cat([pick(DH, head, local_bits + 1 + j, width) for j in range(cross_bits)], 0)
    tokens = q_ref.shape[0]
    step = min(2 * C, tokens)
    for start in range(0, tokens, step):
        here = slice(start, start + step)
        q32 = q_ref[here, :].astype(F32)
        columns = [
            wr[here, local_bits + 1 + j : local_bits + 2 + j] for j in range(cross_bits)
        ]
        att = att_in[here, :].astype(F32) + nn(cat([(w * q32).astype(BF) for w in columns], 1), read)
        back = nt(g_ref[here, :], read)
        dq = dq_in[here, :].astype(F32)
        marks = []
        for j, w in enumerate(columns):
            part = back[:, j * DH : (j + 1) * DH]
            dq = dq + w * part
            marks.append((q32 * part).astype(BF))
        acc[here, :] += nn(cat(marks, 1), picks)
        att_ref[here, :] = att.astype(BF)
        dq_ref[here, :] = dq.astype(BF)
        dk_ref[here, :] = (dk_in[here, :].astype(F32) + nn(v_ref[here, :], adj)).astype(BF)
        dv_ref[here, :] = (dv_in[here, :].astype(F32) + nt(k_ref[here, :], adj)).astype(BF)

    @pl.when(head == pl.num_programs(0) - 1)
    def _():
        gw_ref[...] = acc[...].astype(BF)


def cross_call(query, key, value, grad_out, weights, partial, gws, states, adjoint, local_bits):
    tokens = query.shape[0]
    heads = query.shape[1] // DH
    cross_bits = len(states)
    column = pl.BlockSpec((tokens, DH), lambda h: (0, h))
    whole = pl.BlockSpec(weights.shape, lambda h: (0, 0))
    square = pl.BlockSpec((1, DH, DH), lambda h: (h, 0, 0))
    return pl.pallas_call(
        functools.partial(cross_kernel, local_bits, cross_bits, len(gws)),
        grid=(heads,),
        in_specs=[column] * 4
        + [whole]
        + [column] * 4
        + [whole] * len(gws)
        + [square] * (cross_bits + 1),
        out_specs=[column] * 4 + [whole],
        out_shape=[jax.ShapeDtypeStruct(query.shape, BF)] * 4
        + [jax.ShapeDtypeStruct(weights.shape, BF)],
        scratch_shapes=[pltpu.VMEM(weights.shape, F32), pltpu.VMEM(weights.shape, F32)],
        input_output_aliases={5 + i: i for i in range(4)},
        compiler_params=pltpu.CompilerParams(vmem_limit_bytes=VMEM_LIMIT),
        name="cross",
    )(query, key, value, grad_out, weights, *partial, *gws, *states, adjoint)


def shards(query, key, value, grad_out, weights):
    tokens = query.shape[0]
    heads = query.shape[1] // DH
    local_bits = (tokens // C).bit_length() - 1
    cross_bits = LEVELS - 1 - local_bits
    head_bits = lax.axis_size("head").bit_length() - 1
    sums = sums_call(query, key, value, grad_out, weights, heads, local_bits, cross_bits)
    outs = local_call(query, key, value, grad_out, weights, sums, head_bits)
    partial, gw = outs[:4], outs[4]
    states, adjoint = outs[5 : 5 + cross_bits], outs[5 + cross_bits]
    return tuple(
        cross_call(
            query, key, value, grad_out, weights, partial, [gw], states, adjoint, local_bits
        )
    )


def solution(mesh):
    spec = P(("rep", "seq", "head"), None)
    return jax.shard_map(
        shards, mesh=mesh, in_specs=(spec,) * 5, out_specs=(spec,) * 5, check_vma=False
    )
```

```python
import functools
import math

import jax
import jax.numpy as jnp
from jax import lax
from jax.experimental import pallas as pl
from jax.experimental.pallas import tpu as pltpu
from jax.sharding import PartitionSpec as P

DH = 128
C = 128
LEVELS = 8
VMEM_LIMIT = 60 * 2**20
BF = jnp.bfloat16
F32 = jnp.float32


def level_scale(level):
    if level == 0:
        return 1.0 / math.sqrt(DH * C)
    return 1.0 / math.sqrt(DH * C * 2 ** (level - 1))


def nn(a, b):
    return lax.dot_general(a, b, (((1,), (0,)), ((), ())), preferred_element_type=F32)


def nt(a, b):
    return lax.dot_general(a, b, (((1,), (1,)), ((), ())), preferred_element_type=F32)


def tn(a, b):
    return lax.dot_general(a, b, (((0,), (0,)), ((), ())), preferred_element_type=F32)


def cat(parts, axis):
    return parts[0] if len(parts) == 1 else jnp.concatenate(parts, axis=axis)


def head_weights(w_ref, head):
    width = w_ref.shape[1]
    return pltpu.roll(w_ref[...].astype(F32), lax.rem(width - head * LEVELS, width), 1)


def pick(rows, head, level, width):
    lane = lax.broadcasted_iota(jnp.int32, (rows, width), 1)
    return jnp.where(lane == head * LEVELS + level, 1.0, 0.0).astype(BF)


def sums_kernel(local_bits, q_ref, k_ref, v_ref, g_ref, w_ref, t_ref, *rest):
    p_refs, wr = rest[:-1], rest[-1]
    head = pl.program_id(0)
    wr[...] = head_weights(w_ref, head)
    t_ref[0] = tn(k_ref[...], v_ref[...]).astype(BF)
    q = q_ref[...].astype(F32)
    weighted = [
        (wr[:, local_bits + 1 + j : local_bits + 2 + j] * q).astype(BF) for j in range(len(p_refs))
    ]
    out = tn(g_ref[...], cat(weighted, 1))
    for j, p_ref in enumerate(p_refs):
        p_ref[0] = out[:, j * DH : (j + 1) * DH].astype(BF)


def sums_call(query, key, value, grad_out, weights, heads, local_bits, cross_bits):
    tokens = query.shape[0]
    column = pl.BlockSpec((tokens, DH), lambda h: (0, h))
    square = pl.BlockSpec((1, DH, DH), lambda h: (h, 0, 0))
    outs = [jax.ShapeDtypeStruct((heads, DH, DH), BF)] * (1 + cross_bits)
    return pl.pallas_call(
        functools.partial(sums_kernel, local_bits),
        grid=(heads,),
        in_specs=[column] * 4 + [pl.BlockSpec(weights.shape, lambda h: (0, 0))],
        out_specs=[square] * (1 + cross_bits),
        out_shape=outs,
        scratch_shapes=[pltpu.VMEM(weights.shape, F32)],
        compiler_params=pltpu.CompilerParams(vmem_limit_bytes=VMEM_LIMIT),
        name="sums",
    )(query, key, value, grad_out, weights)


class Exchange:
    def __init__(self, local_bits, cross_bits, head_bits, heads, chunks):
        self.local_bits, self.cross_bits, self.head_bits = local_bits, cross_bits, head_bits
        self.chunks, self.count, self.heads = chunks, heads // chunks, heads
        self.size = 1 << head_bits
        low, high = range(head_bits), range(head_bits, cross_bits)
        self.low, self.high = low, high
        landing = [("R", i) for i in low] + [("PR", j) for j in high]
        landing += [("L", i) for i in low] + [("TL", 0)] + [("PL", j) for j in high]
        landing += [("T", i) for i in high] + [(("P", j), i) for j in high for i in high if i <= j]
        sending = [("TR", 0)] + [("PR", j) for j in high]
        sending += [("L", i) for i in low] + [("TL", 0)] + [("PL", j) for j in high]
        sending += [("T", i) for i in high] + [(("P", j), i) for j in high for i in high if i <= j]
        self.lands = {key: n for n, key in enumerate(landing)}
        self.sends = {key: n for n, key in enumerate(sending)}
        self.last_time = chunks - 1 + self.size + 1 + 2 * (len(high) - 1)

    def scratch(self):
        sems = pltpu.SemaphoreType.DMA((len(self.lands), self.chunks))
        return [
            pltpu.VMEM((len(self.lands), self.heads, DH, DH), BF),
            pltpu.VMEM((len(self.sends), self.heads, DH, DH), BF),
            pltpu.VMEM((self.heads, DH, DH), F32),
            sems,
            sems,
        ]

    def bind(self, sources, states, adjoint, scratch):
        self.total, self.products = sources[0], sources[1:]
        self.states, self.adjoint = states, adjoint
        self.landing, self.sending, self.sum, self.send_sem, self.recv_sem = scratch
        self.z, seq = lax.axis_index("head"), lax.axis_index("seq")
        self.bit = []
        for i in range(self.cross_bits):
            position, stride = self.z, 1 << i
            if i >= self.head_bits:
                position, stride = seq, 1 << (i - self.head_bits)
            self.bit.append((position // stride) % 2)
        self.partner = {
            i: {"seq": seq + (1 - 2 * self.bit[i]) * (1 << (i - self.head_bits))}
            for i in self.high
        }
        self.right, self.left = {"head": self.z + 1}, {"head": self.z - 1}
        self.has_right, self.has_left = self.z < self.size - 1, self.z > 0

    def part(self, chunk):
        return pl.ds(chunk * self.count, self.count)

    def landed(self, key, chunk):
        return self.landing[self.lands[key], self.part(chunk)].astype(F32)

    def store(self, key, chunk, value):
        self.sending[self.sends[key], self.part(chunk)] = value.astype(BF)

    def copy(self, key, chunk, device, source=None):
        slot = self.lands[key]
        if source is None:
            source = self.sending.at[self.sends[key]]
        return pltpu.make_async_remote_copy(
            src_ref=source.at[self.part(chunk)],
            dst_ref=self.landing.at[slot, self.part(chunk)],
            send_sem=self.send_sem.at[slot, chunk],
            recv_sem=self.recv_sem.at[slot, chunk],
            device_id=device,
            device_id_type=pl.DeviceIdType.MESH,
        )

    def transfers(self):
        for i in self.low:
            yield ("R", i), self.right, self.has_right & (((self.z + 1) >> i) % 2 == 1), self.bit[i] == 1
        for j in self.high:
            own = self.bit[j] == 1
            yield ("PR", j), self.right, self.has_right & own, self.has_left & own
        for i in self.low:
            block = self.z % (2 << i)
            yield ("L", i), self.left, block != 0, block != (2 << i) - 1
        yield ("TL", 0), self.left, self.has_left, self.has_right
        for j in self.high:
            own = self.bit[j] == 1
            yield ("PL", j), self.left, self.has_left & own, self.has_right & own
        for i in self.high:
            up, down, always = self.bit[i] == 1, self.bit[i] == 0, self.bit[i] >= 0
            last = i == self.cross_bits - 1
            yield ("T", i), self.partner[i], (down if last else always), (up if last else always)
            yield (("P", i), i), self.partner[i], up, down
            for j in range(i + 1, self.cross_bits):
                own = self.bit[j] == 1
                yield (("P", j), i), self.partner[i], own, own

    def greet(self):
        barrier = pltpu.get_barrier_semaphore()

        def signal(device):
            pl.semaphore_signal(
                barrier, inc=1, device_id=device, device_id_type=pl.DeviceIdType.MESH
            )

        for i in self.high:
            signal(self.partner[i])
        signal({"head": lax.rem(self.z + 1, self.size)})
        signal({"head": lax.rem(self.z + self.size - 1, self.size)})
        pl.semaphore_wait(barrier, len(self.high) + 2)

    def wait(self, chunk, kinds):
        for key, device, _, receives in self.transfers():
            if key in kinds:
                own = self.landing.at[self.lands[key]]
                pl.when(receives)(
                    lambda k=key, d=device, r=own: self.copy(k, chunk, d, r).wait_recv()
                )

    def start(self, chunk, kinds):
        for key, device, sends, _ in self.transfers():
            if key in kinds:
                pl.when(sends)(lambda k=key, d=device: self.copy(k, chunk, d).start())

    def chain(self, key, chunk, own, receives):
        @pl.when(receives)
        def _():
            self.store(key, chunk, own.astype(F32) + self.landed(key, chunk))

        @pl.when(jnp.logical_not(receives))
        def _():
            self.store(key, chunk, own)

    def rightward(self, chunk):
        part = self.part(chunk)
        self.wait(chunk, [("R", i) for i in self.low] + [("PR", j) for j in self.high])
        for i in self.low:
            @pl.when(self.z % (2 << i) == (1 << i) - 1)
            def _(i=i):
                value = self.total[part].astype(F32)
                for k in range(i):
                    value = value + self.landed(("R", k), chunk)
                self.store(("TR", 0), chunk, value)
                self.copy(
                    ("R", i), chunk, self.right, self.sending.at[self.sends["TR", 0]]
                ).start()

            @pl.when((self.bit[i] == 1) & (self.z % (1 << i) != (1 << i) - 1))
            def _(i=i):
                self.copy(
                    ("R", i), chunk, self.right, self.landing.at[self.lands["R", i]]
                ).start()

        for j in self.high:

            @pl.when((self.bit[j] == 1) & self.has_right)
            def _(j=j):
                self.chain(("PR", j), chunk, self.products[j][part], self.has_left)

        self.start(chunk, [("PR", j) for j in self.high])

    def leftward(self, chunk):
        part = self.part(chunk)
        keys = [("L", i) for i in self.low] + [("TL", 0)] + [("PL", j) for j in self.high]
        self.wait(chunk, keys)
        for i in self.low:
            block = self.z % (2 << i)

            @pl.when(self.bit[i] == 1)
            def _(i=i, block=block):
                self.chain(("L", i), chunk, self.products[i][part], block != (2 << i) - 1)
                self.copy(("L", i), chunk, self.left).start()

            @pl.when((self.bit[i] == 0) & (block != 0))
            def _(i=i):
                self.copy(("L", i), chunk, self.left, self.landing.at[self.lands["L", i]]).start()

        @pl.when(self.has_left)
        def _():
            self.chain(("TL", 0), chunk, self.total[part], self.has_right)

        for j in self.high:

            @pl.when((self.bit[j] == 1) & self.has_left)
            def _(j=j):
                self.chain(("PL", j), chunk, self.products[j][part], self.has_right)

        self.start(chunk, [("TL", 0)] + [("PL", j) for j in self.high])

    def add(self, key, chunk, source, receives, first=None):
        @pl.when(receives)
        def _():
            base = self.sending[self.sends[first or key], self.part(chunk)].astype(F32)
            self.store(key, chunk, base + self.landed(source, chunk))

    def read(self, i, chunk, state, term):
        part = self.part(chunk)
        factor = level_scale(self.local_bits + i + 1)

        @pl.when(self.bit[i] == 1)
        def _():
            self.states[i][part] = (factor * self.landed(state, chunk)).astype(BF)

        @pl.when(self.bit[i] == 0)
        def _():
            self.states[i][part] = jnp.zeros((self.count, DH, DH), BF)
            self.sum[part] += factor * self.landed(term, chunk)

    def cross(self, chunk):
        part = self.part(chunk)
        self.sum[part] = jnp.zeros((self.count, DH, DH), F32)
        for i in self.low:
            self.read(i, chunk, ("R", i), ("L", i))
        first = self.head_bits
        value = self.total[part].astype(F32)
        for i in self.low:
            value = value + jnp.where(self.bit[i] == 1, self.landed(("R", i), chunk), 0.0)
        value = value + jnp.where(self.has_right, self.landed(("TL", 0), chunk), 0.0)
        self.store(("T", first), chunk, value)
        for j in self.high:

            @pl.when(self.bit[j] == 1)
            def _(j=j):
                value = self.products[j][part].astype(F32)
                value = value + jnp.where(self.has_left, self.landed(("PR", j), chunk), 0.0)
                value = value + jnp.where(self.has_right, self.landed(("PL", j), chunk), 0.0)
                self.store((("P", j), first), chunk, value)

        self.start(chunk, [("T", first)] + [(("P", j), first) for j in self.high])

    def arrive(self, i, chunk):
        part = self.part(chunk)
        above = range(i + 1, self.cross_bits)
        self.wait(chunk, [("T", i), (("P", i), i)] + [(("P", j), i) for j in above])
        if len(above):
            self.add(("T", i + 1), chunk, ("T", i), self.bit[i] >= 0, ("T", i))
            for j in above:
                self.add((("P", j), i + 1), chunk, (("P", j), i), self.bit[j] == 1, (("P", j), i))
            self.start(chunk, [("T", i + 1)] + [(("P", j), i + 1) for j in above])
        self.read(i, chunk, ("T", i), (("P", i), i))
        if not len(above):
            self.adjoint[part] = self.sum[part].astype(BF)

    def advance(self, time):
        def at(offset, event):
            chunk = time - offset

            @pl.when((chunk >= 0) & (chunk < self.chunks))
            def _():
                event(chunk)

        at(self.z, self.rightward)
        at(self.size - 1 - self.z, self.leftward)
        at(self.size - 1, self.cross)
        for i in self.high:
            at(self.size + 1 + 2 * (i - self.head_bits), functools.partial(self.arrive, i))

    def finish(self, steps):
        def late(time, carry):
            self.advance(time)
            return carry

        if self.last_time >= steps:
            lax.fori_loop(steps, self.last_time + 1, late, 0)

        def body(chunk, carry):
            for key, device, sends, _ in self.transfers():
                source = self.landing.at[self.lands[key]]
                pl.when(sends)(
                    lambda k=key, d=device, r=source: self.copy(k, chunk, d, r).wait_send()
                )
            return carry

        lax.fori_loop(0, self.chunks, body, 0)


def local_kernel(stretches, exchange, *refs):
    cross_bits = exchange.cross_bits
    q_ref, k_ref, v_ref, g_ref, w_ref = refs[:5]
    sources = refs[5 : 6 + cross_bits]
    outs = refs[6 + cross_bits :]
    att_ref, dq_ref, dk_ref, dv_ref, gw_ref = outs[:5]
    states_out = outs[5 : 5 + cross_bits]
    adjoint_out, wr = outs[5 + cross_bits : 7 + cross_bits]
    exchange.bind(sources, states_out, adjoint_out, outs[7 + cross_bits :])
    step = pl.program_id(0)
    head = step
    local_bits = stretches.bit_length() - 1
    width = w_ref.shape[1]

    @pl.when(step == 0)
    def _():
        gw_ref[...] = jnp.zeros_like(gw_ref)

    pl.when(step == 0)(exchange.greet)
    exchange.advance(step)
    wr[...] = head_weights(w_ref, head)

    def rows(ref, n, count=1):
        return ref[n * C : (n + count) * C, :]

    def weighted(n, level):
        return (wr[n * C : (n + 1) * C, level : level + 1] * rows(q_ref, n).astype(F32)).astype(BF)

    sums = {}
    for n in range(stretches - 1):
        sums[0, n] = tn(rows(k_ref, n), rows(v_ref, n))
    for b in range(1, local_bits):
        for m in range(stretches >> b):
            if (b - 1, 2 * m + 1) in sums:
                sums[b, m] = sums[b - 1, 2 * m] + sums[b - 1, 2 * m + 1]
    states, adjoints, wq = {}, {}, {}
    for b in range(local_bits):
        for group in range(stretches >> (b + 1)):
            states[b, group] = (level_scale(b + 1) * sums[b, 2 * group]).astype(BF)
            first = (2 * group + 1) << b
            for n in range(first, first + (1 << b)):
                wq[b, n] = weighted(n, b + 1)
            up = cat([wq[b, n] for n in range(first, first + (1 << b))], 0)
            adjoints[b, group] = level_scale(b + 1) * tn(rows(g_ref, first, 1 << b), up)

    row = lax.broadcasted_iota(jnp.int32, (C, C), 0)
    col = lax.broadcasted_iota(jnp.int32, (C, C), 1)
    mask = jnp.where(col <= row, level_scale(0), 0.0).astype(F32)
    for n in range(stretches):
        q, k, v, g = (rows(ref, n) for ref in (q_ref, k_ref, v_ref, g_ref))
        here = slice(n * C, (n + 1) * C)
        bits = [b for b in range(local_bits) if n >> b & 1]
        read = [states[b, n >> (b + 1)] for b in bits]
        scores = nt(q, k) * mask
        grads = nt(g, v)
        w0 = wr[here, 0:1]
        probs = (w0 * scores).astype(BF)
        gscores = (w0 * (grads * mask)).astype(BF)
        att = nn(cat([probs] + [wq[b, n] for b in bits], 1), cat([v] + read, 0))
        dq = nn(gscores, k)
        marks = [(scores * grads).astype(BF)]
        q32 = q.astype(F32)
        for b, state in zip(bits, read):
            back = nt(g, state)
            dq = dq + wr[here, b + 1 : b + 2] * back
            marks.append((q32 * back).astype(BF))
        picks = [pick(C, head, level, width) for level in [0] + [b + 1 for b in bits]]
        gw_ref[here, :] += nn(cat(marks, 1), cat(picks, 0))
        dk = tn(gscores, q)
        dv = tn(probs, g)
        adjoint = None
        for b in range(local_bits):
            if not n >> b & 1:
                term = adjoints[b, n >> (b + 1)]
                adjoint = term if adjoint is None else adjoint + term
        if adjoint is not None:
            adjoint = adjoint.astype(BF)
            dk = dk + nn(v, adjoint)
            dv = dv + nt(k, adjoint)
        att_ref[here, :] = att.astype(BF)
        dq_ref[here, :] = dq.astype(BF)
        dk_ref[here, :] = dk.astype(BF)
        dv_ref[here, :] = dv.astype(BF)

    @pl.when(step == pl.num_programs(0) - 1)
    def _():
        exchange.finish(exchange.heads)


def local_call(query, key, value, grad_out, weights, sums, head_bits):
    tokens = query.shape[0]
    stretches = tokens // C
    heads = query.shape[1] // DH
    cross_bits = len(sums) - 1
    exchange = Exchange(stretches.bit_length() - 1, cross_bits, head_bits, heads, heads // 2)
    column = pl.BlockSpec((tokens, DH), lambda h: (0, h))
    whole = pl.BlockSpec(weights.shape, lambda h: (0, 0))
    squares = pl.BlockSpec((heads, DH, DH), lambda h: (0, 0, 0))
    shape = jax.ShapeDtypeStruct(query.shape, BF)
    square = jax.ShapeDtypeStruct((heads, DH, DH), BF)
    return pl.pallas_call(
        functools.partial(local_kernel, stretches, exchange),
        grid=(heads,),
        in_specs=[column] * 4 + [whole] + [squares] * (cross_bits + 1),
        out_specs=[column] * 4 + [whole] + [squares] * (cross_bits + 1),
        out_shape=[shape] * 4
        + [jax.ShapeDtypeStruct(weights.shape, F32)]
        + [square] * (cross_bits + 1),
        scratch_shapes=[pltpu.VMEM(weights.shape, F32)] + exchange.scratch(),
        compiler_params=pltpu.CompilerParams(
            vmem_limit_bytes=VMEM_LIMIT, collective_id=0, has_side_effects=True
        ),
        name="local",
    )(query, key, value, grad_out, weights, *sums)


def cross_kernel(local_bits, cross_bits, chunks, *refs):
    q_ref, k_ref, v_ref, g_ref, w_ref = refs[:5]
    att_in, dq_in, dk_in, dv_in = refs[5:9]
    gw_in = refs[9 : 9 + chunks]
    states = refs[9 + chunks : 9 + chunks + cross_bits]
    adjoint = refs[9 + chunks + cross_bits]
    att_ref, dq_ref, dk_ref, dv_ref, gw_ref, acc, wr = refs[10 + chunks + cross_bits :]
    head = pl.program_id(0)
    width = w_ref.shape[1]

    @pl.when(head == 0)
    def _():
        total = gw_in[0][...]
        for other in gw_in[1:]:
            total = total + other[...]
        acc[...] = total

    wr[...] = head_weights(w_ref, head)
    read = cat([state[0] for state in states], 0)
    adj = adjoint[0]
    picks = cat([pick(DH, head, local_bits + 1 + j, width) for j in range(cross_bits)], 0)
    tokens = q_ref.shape[0]
    step = min(2 * C, tokens)
    for start in range(0, tokens, step):
        here = slice(start, start + step)
        q32 = q_ref[here, :].astype(F32)
        columns = [
            wr[here, local_bits + 1 + j : local_bits + 2 + j] for j in range(cross_bits)
        ]
        att = att_in[here, :].astype(F32) + nn(cat([(w * q32).astype(BF) for w in columns], 1), read)
        back = nt(g_ref[here, :], read)
        dq = dq_in[here, :].astype(F32)
        marks = []
        for j, w in enumerate(columns):
            part = back[:, j * DH : (j + 1) * DH]
            dq = dq + w * part
            marks.append((q32 * part).astype(BF))
        acc[here, :] += nn(cat(marks, 1), picks)
        att_ref[here, :] = att.astype(BF)
        dq_ref[here, :] = dq.astype(BF)
        dk_ref[here, :] = (dk_in[here, :].astype(F32) + nn(v_ref[here, :], adj)).astype(BF)
        dv_ref[here, :] = (dv_in[here, :].astype(F32) + nt(k_ref[here, :], adj)).astype(BF)

    @pl.when(head == pl.num_programs(0) - 1)
    def _():
        gw_ref[...] = acc[...].astype(BF)


def cross_call(query, key, value, grad_out, weights, partial, gws, states, adjoint, local_bits):
    tokens = query.shape[0]
    heads = query.shape[1] // DH
    cross_bits = len(states)
    column = pl.BlockSpec((tokens, DH), lambda h: (0, h))
    whole = pl.BlockSpec(weights.shape, lambda h: (0, 0))
    square = pl.BlockSpec((1, DH, DH), lambda h: (h, 0, 0))
    return pl.pallas_call(
        functools.partial(cross_kernel, local_bits, cross_bits, len(gws)),
        grid=(heads,),
        in_specs=[column] * 4
        + [whole]
        + [column] * 4
        + [whole] * len(gws)
        + [square] * (cross_bits + 1),
        out_specs=[column] * 4 + [whole],
        out_shape=[jax.ShapeDtypeStruct(query.shape, BF)] * 4
        + [jax.ShapeDtypeStruct(weights.shape, BF)],
        scratch_shapes=[pltpu.VMEM(weights.shape, F32), pltpu.VMEM(weights.shape, F32)],
        compiler_params=pltpu.CompilerParams(vmem_limit_bytes=VMEM_LIMIT),
        name="cross",
    )(query, key, value, grad_out, weights, *partial, *gws, *states, adjoint)


def shards(query, key, value, grad_out, weights):
    tokens = query.shape[0]
    heads = query.shape[1] // DH
    local_bits = (tokens // C).bit_length() - 1
    cross_bits = LEVELS - 1 - local_bits
    head_bits = lax.axis_size("head").bit_length() - 1
    sums = sums_call(query, key, value, grad_out, weights, heads, local_bits, cross_bits)
    outs = local_call(query, key, value, grad_out, weights, sums, head_bits)
    partial, gw = outs[:4], outs[4]
    states, adjoint = outs[5 : 5 + cross_bits], outs[5 + cross_bits]
    return tuple(
        cross_call(
            query, key, value, grad_out, weights, partial, [gw], states, adjoint, local_bits
        )
    )


def solution(mesh):
    spec = P(("rep", "seq", "head"), None)
    return jax.shard_map(
        shards, mesh=mesh, in_specs=(spec,) * 5, out_specs=(spec,) * 5, check_vma=False
    )
```
